256 devices in a mesh: row: 16 (over y, z_hi, core), col: 16 (over x, z_lo).
Axes of the slice: x: 4, y: 4, z: 8 (z_hi: 2, z_lo: 4; z = z_hi * 4 + z_lo), core: 2. Of those that a mesh axis runs over, the one named last changes fastest.
Arguments:
- eigvec: float32 [16384, 20480], P('row', 'col'), may hold values from -6 to 6
- panels: float32 [3, 16384, 256], P(None, ('row', 'col')), may hold values from -0.375 to 0.375
- factors: float32 [3, 256, 256], replicated, may hold values from -0.046875 to 0.046875
Outputs:
- updated: float32 [16384, 20480], P('row', 'col')
The draws below stay inside these ranges and needn't reach their ends.
All inputs are finite; a program needn't handle non-finite values.
Results may differ from the reference program's by a relative error of at most 0.00012.
Values sent between devices are 32-bit elements; how exact they have to be, the bound alone decides.
No kernel may reach another device: no remote copies, remote signals or barrier semaphores. Data moves between devices by JAX's collectives and lax.ppermute only.
A program may use at most 64 MiB of HBM per device.

```python
import jax
import jax.numpy as jnp
from jax import lax

NB = 256
NREF = 3
ROWS = 16384
COLS = 20480


def levels(key, extent, shards, least, high):
    def one(dim, parts):
        draws = jax.random.uniform(jax.random.fold_in(jax.random.fold_in(key, 6), dim), (parts,), jnp.float32, least / len(shards), high / len(shards))
        return jnp.repeat(jnp.exp(draws), extent[dim] // parts).reshape((-1,) + (1,) * (len(extent) - dim - 1))

    loudness = one(*shards[0])
    for cut in shards[1:]:
        loudness = loudness * one(*cut)
    return loudness


def bell_draw(key, extent, scale, bound, split=(), held_as=jnp.bfloat16):
    result = jax.random.normal(key, extent, jnp.float32) * scale
    if len(split) > 0:
        result = levels(key, extent, split, -0.22, 0.18) * result
    return jnp.clip(result, min=-bound, max=bound).astype(held_as)


def setup_inputs(seed: int = 0) -> dict:
    key_of = jax.random.split(jax.random.key(seed), 4)
    eigvec = bell_draw(key_of[0], (ROWS, COLS), 1.0, 6.0, ((0, 16), (1, 16)), jnp.float32)
    panels = bell_draw(key_of[1], (NREF, ROWS, NB), NB ** -0.5, 0.375, ((1, 256),), jnp.float32)
    factors = bell_draw(key_of[2], (NREF, NB, NB), ROWS ** -0.5, 0.046875, (), jnp.float32)
    return dict(eigvec=eigvec, panels=panels, factors=factors)


def reference(eigvec, panels, factors):
    highest = lax.Precision.HIGHEST
    upper = jnp.triu(factors)
    field = eigvec
    for index in range(NREF):
        coeff = jnp.dot(panels[index].T, field, precision=highest, preferred_element_type=jnp.float32)
        scaled = jnp.dot(upper[index], coeff, precision=highest, preferred_element_type=jnp.float32)
        field = field - jnp.dot(panels[index], scaled, precision=highest, preferred_element_type=jnp.float32)
    return field
```

```python
import functools

import jax
import jax.numpy as jnp
import numpy as np
from jax import lax
from jax.experimental import pallas as pl
from jax.experimental.pallas import tpu as pltpu
from jax.sharding import PartitionSpec as P

NREF = 3
BF = jnp.bfloat16
F32 = jnp.float32


def lin(y, zh, c, x, zl):
    return ((y * 2 + zh) * 2 + c) * 16 + x * 4 + zl


def xor_pair(core):
    return (1, 3) if core == 0 else (3, 1)


def perm_of(f):
    pairs = []
    for y in range(4):
        for zh in range(2):
            for c in range(2):
                for x in range(4):
                    for zl in range(4):
                        pairs.append((lin(y, zh, c, x, zl), lin(*f(y, zh, c, x, zl))))
    return pairs


CORE = perm_of(lambda y, zh, c, x, zl: (y, zh, 1 - c, x, zl))
Y1 = perm_of(lambda y, zh, c, x, zl: (y ^ xor_pair(c)[0], zh, c, x, zl))
Y2 = perm_of(lambda y, zh, c, x, zl: (y ^ xor_pair(c)[1], zh, c, x, zl))
X1 = perm_of(lambda y, zh, c, x, zl: (y, zh, c, x ^ xor_pair(c)[0], zl))
X2 = perm_of(lambda y, zh, c, x, zl: (y, zh, c, x ^ xor_pair(c)[1], zl))
ZH = perm_of(lambda y, zh, c, x, zl: (y, 1 - zh, c, x, zl))
ZL = [perm_of(lambda y, zh, c, x, zl, d=d: (y, zh, c, x, zl ^ d)) for d in range(4)]


def send(a, perm):
    return lax.ppermute(a, ("row", "col"), perm)


def tables():
    piece = np.zeros((16, 8), np.int32)
    block = np.zeros((2, 16, 16), np.int32)
    for r in range(16):
        y, c = r // 4, r % 2
        for p in range(8):
            b0, b1, b2 = p // 4, (p // 2) % 2, p % 2
            owner = c ^ b0
            g = xor_pair(owner)
            piece[r, p] = owner * 4 + (y ^ (b1 * g[0]) ^ (b2 * g[1]))
    for c in range(2):
        g = xor_pair(c)
        for j in range(16):
            x, zl = j // 4, j % 4
            for p in range(16):
                b2, b1, zp = p // 8, (p // 4) % 2, p % 4
                block[c, j, p] = (x ^ (b1 * g[0]) ^ (b2 * g[1])) * 4 + (zl ^ zp)
    return piece, block


def split(v):
    hi = v.astype(BF)
    return hi, (v - hi.astype(F32)).astype(BF)


def dot3(ah, al, bh, bl, dims=(((1,), (0,)), ((), ()))):
    d = functools.partial(lax.dot_general, dimension_numbers=dims, preferred_element_type=F32)
    return d(ah, bh) + (d(ah, bl) + d(al, bh))


def prep_kernel(piece, field_ref, hi_ref, lo_ref, buf):
    n = field_ref.shape[1]
    w = n // 8
    buf[...] = field_ref[...].T
    for p in range(8):
        q = piece[p]
        v = buf[pl.ds(pl.multiple_of(q * w, 16), w), :]
        h, l = split(v)
        hi_ref[p * w:(p + 1) * w, :] = h
        lo_ref[p * w:(p + 1) * w, :] = l


def prep(piece, field):
    rows, cols = field.shape
    return pl.pallas_call(
        prep_kernel,
        out_shape=[jax.ShapeDtypeStruct((cols, rows), BF)] * 2,
        in_specs=[pl.BlockSpec(memory_space=pltpu.SMEM), pl.BlockSpec(memory_space=pltpu.VMEM)],
        out_specs=[pl.BlockSpec(memory_space=pltpu.VMEM)] * 2,
        scratch_shapes=[pltpu.VMEM((cols, rows), F32)],
        compiler_params=pltpu.CompilerParams(vmem_limit_bytes=24 << 20),
        cost_estimate=pl.CostEstimate(flops=0, bytes_accessed=rows * cols * 8, transcendentals=0),
        name="prep",
    )(piece, field)


def project_kernel(k, last, *refs):
    piece, block, b_ref, c_ref, hi_ref, lo_ref = refs[:6]
    prev = refs[6:6 + 2 * k]
    outs = refs[6 + 2 * k:]
    keep_ref, give_ref, vh_ref, vl_ref = outs[:4]
    vbuf = outs[-1]
    half = b_ref.shape[0]
    for p in range(16):
        src = b_ref if p < 8 else c_ref
        v = src[(p % 8) * (half // 8):(p % 8 + 1) * (half // 8), :]
        vbuf[pl.ds(pl.multiple_of(block[p] * (half // 8), 64), half // 8), :] = v
    vh_ref[...], vl_ref[...] = split(vbuf[...])
    vh, vl = vh_ref[...], vl_ref[...]
    w = hi_ref.shape[0] // 8
    r = w + 32 * k
    for h, out in ((1, give_ref), (0, keep_ref)):
        a = slice(h * 4 * w, (h + 1) * 4 * w)
        res = dot3(hi_ref[a, :], lo_ref[a, :], vh, vl)
        for p in range(4):
            out[p * r:p * r + w, :] = res[p * w:(p + 1) * w, :]
        for j in range(k):
            a = slice(h * 128, (h + 1) * 128)
            res = dot3(prev[2 * j][a, :], prev[2 * j + 1][a, :], vh, vl)
            for p in range(4):
                o = p * r + w + 32 * j
                out[o:o + 32, :] = res[p * 32:(p + 1) * 32, :]
    if not last:
        th_ref, tl_ref = outs[4:6]
        vt = vbuf[...].T
        vbuf[0:256, :] = vt[:, 0:256]
        vbuf[256:512, :] = vt[:, 256:512]
        vbuf[512:768, :] = vt[:, 512:768]
        vbuf[768:1024, :] = vt[:, 768:1024]
        for p in range(8):
            for m in range(4):
                v = vbuf[pl.ds(pl.multiple_of(m * 256 + piece[p] * 32, 32), 32), :]
                h, l = split(v)
                th_ref[p * 32:(p + 1) * 32, m * 256:(m + 1) * 256] = h
                tl_ref[p * 32:(p + 1) * 32, m * 256:(m + 1) * 256] = l


def project(k, piece, block, b, c, hi, lo, prev):
    last = k == NREF - 1
    rows, nb = 2 * b.shape[0], b.shape[1]
    cols = hi.shape[0]
    r = cols // 8 + 32 * k
    out = [jax.ShapeDtypeStruct((4 * r, nb), F32)] * 2 + [jax.ShapeDtypeStruct((rows, nb), BF)] * 2
    if not last:
        out += [jax.ShapeDtypeStruct((nb, rows), BF)] * 2
    vmem = pl.BlockSpec(memory_space=pltpu.VMEM)
    smem = pl.BlockSpec(memory_space=pltpu.SMEM)
    return pl.pallas_call(
        functools.partial(project_kernel, k, last),
        out_shape=out,
        in_specs=[smem, smem] + [vmem] * (4 + 2 * k),
        out_specs=[vmem] * len(out),
        scratch_shapes=[pltpu.VMEM((rows, nb), F32)],
        compiler_params=pltpu.CompilerParams(vmem_limit_bytes=24 << 20),
        cost_estimate=pl.CostEstimate(flops=6 * 8 * r * rows * nb, bytes_accessed=4 * rows * cols + 8 * rows * nb, transcendentals=0),
        name=f"project{k}",
    )(piece, block, b, c, hi, lo, *prev)


def update_kernel(k, last, *refs):
    piece, own_ref, got_ref, vh_ref, vl_ref, t_ref, field_ref = refs[:7]
    prev = refs[7:7 + 2 * k]
    outs = refs[7 + 2 * k:]
    out_ref, sh_ref, sl_ref = outs[:3]
    w_ref, g_ref = outs[3:5]
    n = pl.program_id(0)
    w = w_ref.shape[0] // 8
    r = w + 32 * k

    @pl.when(n == 0)
    def _():
        for p in range(8):
            src = own_ref if p < 4 else got_ref
            o = (p % 4) * r
            q = piece[p]
            w_ref[pl.ds(pl.multiple_of(q * w, 32), w), :] = src[o:o + w, :]
            for j in range(k):
                a = o + w + 32 * j
                g_ref[pl.ds(pl.multiple_of(j * 256 + q * 32, 32), 32), :] = src[a:a + 32, :]
        coeff = w_ref[...]
        for j in range(k):
            gh, gl = split(g_ref[j * 256:(j + 1) * 256, :])
            coeff = coeff - dot3(prev[2 * j][...], prev[2 * j + 1][...], gh, gl)
        t = t_ref[...]
        at = lax.broadcasted_iota(jnp.int32, t.shape, 0)
        upto = lax.broadcasted_iota(jnp.int32, t.shape, 1)
        th, tl = split(jnp.where(at <= upto, t, 0.0))
        ch, cl = split(coeff)
        s = dot3(ch, cl, th, tl, (((1,), (1,)), ((), ())))
        sh_ref[...], sl_ref[...] = split(s)

    tile = field_ref.shape[1]
    a = pl.ds(pl.multiple_of(n * tile, tile), tile)
    out_ref[...] = field_ref[...] - dot3(vh_ref[...], vl_ref[...], sh_ref[a, :], sl_ref[a, :], (((1,), (1,)), ((), ())))


def update(k, piece, own, got, vh, vl, t, field, prev):
    last = k == NREF - 1
    rows, cols = field.shape
    nb = vh.shape[1]
    tile = 256
    full = lambda a: pl.BlockSpec(a.shape, lambda n: (0, 0))
    smem = pl.BlockSpec(memory_space=pltpu.SMEM)
    cut = pl.BlockSpec((rows, tile), lambda n: (0, n))
    sdef = jax.ShapeDtypeStruct((cols, nb), BF)
    res = pl.pallas_call(
        functools.partial(update_kernel, k, last),
        grid=(cols // tile,),
        out_shape=[jax.ShapeDtypeStruct(field.shape, F32), sdef, sdef],
        in_specs=[smem, full(own), full(got), full(vh), full(vl), full(t), cut] + [full(a) for a in prev],
        out_specs=[cut, full(sdef), full(sdef)],
        scratch_shapes=[pltpu.VMEM((cols, nb), F32), pltpu.VMEM((512, nb), F32)],
        compiler_params=pltpu.CompilerParams(vmem_limit_bytes=32 << 20),
        cost_estimate=pl.CostEstimate(flops=6 * rows * cols * nb, bytes_accessed=8 * rows * cols, transcendentals=0),
        name=f"update{k}",
    )(piece, own, got, vh, vl, t, field, *prev)
    return res


def per_device(eigvec, panels, factors):
    piece_t, block_t = tables()
    row, col = lax.axis_index("row"), lax.axis_index("col")
    piece = jnp.asarray(piece_t)[row]
    block = jnp.asarray(block_t)[row % 2, col]

    def spread(v):
        return [v] + [send(v, ZL[d]) for d in (1, 2, 3)]

    first = spread(panels[0])
    rest = spread(panels[1:])
    hi, lo = prep(piece, eigvec)
    vs, ts, ws = [], [], []
    for k in range(NREF):
        a = jnp.concatenate(first if k == 0 else [v[k - 1] for v in rest], axis=0)
        b = jnp.concatenate([a, send(a, X1)], axis=0)
        c = send(b, X2)
        keep, give, vh, vl, *t = project(k, piece, block, b, c, hi, lo, [u for pair in ts for u in pair])
        vs.append((vh, vl))
        if t:
            ts.append(t)
        w = keep + send(give, CORE)
        h = w.shape[0] // 2
        w = w[:h] + send(w[h:], Y1)
        w = w[:h // 2] + send(w[h // 2:], Y2)
        w = w + send(w, ZH)
        w = jnp.concatenate([w, send(w, Y2)], axis=0)
        w = jnp.concatenate([w, send(w, Y1)], axis=0)
        ws.append((w, send(w, CORE)))
    field = eigvec
    ss = []
    for k in range(NREF):
        field, *s = update(k, piece, *ws[k], *vs[k], factors[k], field, [u for pair in ss for u in pair])
        ss.append(s)
    return field


def solution(mesh):
    in_specs = (P("row", "col"), P(None, ("row", "col"), None), P())
    out_specs = P("row", "col")
    return jax.shard_map(
        per_device, mesh=mesh, in_specs=in_specs, out_specs=out_specs, check_vma=False
    )
```

```python
import functools

import jax
import jax.numpy as jnp
import numpy as np
from jax import lax
from jax.experimental import pallas as pl
from jax.experimental.pallas import tpu as pltpu
from jax.sharding import PartitionSpec as P


NREF = 3
BF = jnp.bfloat16
F32 = jnp.float32


def lin(y, zh, c, x, zl):
    return ((y * 2 + zh) * 2 + c) * 16 + x * 4 + zl


def xor_pair(core):
    return (1, 3) if core == 0 else (3, 1)


def perm_of(f):
    pairs = []
    for y in range(4):
        for zh in range(2):
            for c in range(2):
                for x in range(4):
                    for zl in range(4):
                        pairs.append((lin(y, zh, c, x, zl), lin(*f(y, zh, c, x, zl))))
    return pairs


CORE = perm_of(lambda y, zh, c, x, zl: (y, zh, 1 - c, x, zl))
Y1 = perm_of(lambda y, zh, c, x, zl: (y ^ xor_pair(c)[0], zh, c, x, zl))
Y2 = perm_of(lambda y, zh, c, x, zl: (y ^ xor_pair(c)[1], zh, c, x, zl))
X1 = perm_of(lambda y, zh, c, x, zl: (y, zh, c, x ^ xor_pair(c)[0], zl))
X2 = perm_of(lambda y, zh, c, x, zl: (y, zh, c, x ^ xor_pair(c)[1], zl))
ZH = perm_of(lambda y, zh, c, x, zl: (y, 1 - zh, c, x, zl))
ZL = [perm_of(lambda y, zh, c, x, zl, d=d: (y, zh, c, x, zl ^ d)) for d in range(4)]


def send(a, perm):
    return lax.ppermute(a, ("row", "col"), perm)


def tables():
    piece = np.zeros((16, 8), np.int32)
    block = np.zeros((2, 16, 16), np.int32)
    for r in range(16):
        y, c = r // 4, r % 2
        for p in range(8):
            b0, b1, b2 = p // 4, (p // 2) % 2, p % 2
            owner = c ^ b0
            g = xor_pair(owner)
            piece[r, p] = owner * 4 + (y ^ (b1 * g[0]) ^ (b2 * g[1]))
    for c in range(2):
        g = xor_pair(c)
        for j in range(16):
            x, zl = j // 4, j % 4
            for p in range(16):
                b2, b1, zp = p // 8, (p // 4) % 2, p % 4
                block[c, j, p] = (x ^ (b1 * g[0]) ^ (b2 * g[1])) * 4 + (zl ^ zp)
    return piece, block


def split(v):
    hi = v.astype(BF)
    return hi, (v - hi.astype(F32)).astype(BF)


def dot3(ah, al, bh, bl, dims=(((1,), (0,)), ((), ()))):
    d = functools.partial(lax.dot_general, dimension_numbers=dims, preferred_element_type=F32)
    return d(ah, bh) + (d(ah, bl) + d(al, bh))


def prep_kernel(piece, field_ref, hi_ref, lo_ref, buf):
    w = field_ref.shape[1] // 8
    buf[...] = field_ref[...].T
    for p in range(8):
        v = buf[pl.ds(pl.multiple_of(piece[p] * w, 32), w), :]
        a = slice(p * w, (p + 1) * w)
        hi_ref[a, :], lo_ref[a, :] = split(v)


def prep(piece, field):
    rows, cols = field.shape
    tile = 128
    return pl.pallas_call(
        prep_kernel,
        grid=(rows // tile,),
        out_shape=[jax.ShapeDtypeStruct((cols, rows), BF)] * 2,
        in_specs=[pl.BlockSpec(memory_space=pltpu.SMEM), pl.BlockSpec((tile, cols), lambda n: (n, 0))],
        out_specs=[pl.BlockSpec((cols, tile), lambda n: (0, n))] * 2,
        scratch_shapes=[pltpu.VMEM((cols, tile), F32)],
        compiler_params=pltpu.CompilerParams(vmem_limit_bytes=16 << 20),
        cost_estimate=pl.CostEstimate(flops=0, bytes_accessed=rows * cols * 8, transcendentals=0),
        name="prep",
    )(piece, field)


def project_kernel(k, last, *refs):
    piece, block, b_ref, c_ref, hi_ref, lo_ref = refs[:6]
    prev = refs[6:6 + 2 * k]
    outs = refs[6 + 2 * k:]
    keep_ref, give_ref, vh_ref, vl_ref = outs[:4]
    vbuf = outs[-1]
    half = b_ref.shape[0]
    for p in range(16):
        src = b_ref if p < 8 else c_ref
        v = src[(p % 8) * (half // 8):(p % 8 + 1) * (half // 8), :]
        vbuf[pl.ds(pl.multiple_of(block[p] * (half // 8), 64), half // 8), :] = v
    vh_ref[...], vl_ref[...] = split(vbuf[...])
    vh, vl = vh_ref[...], vl_ref[...]
    w = hi_ref.shape[0] // 8
    r = w + 32 * k
    for h, out in ((1, give_ref), (0, keep_ref)):
        a = slice(h * 4 * w, (h + 1) * 4 * w)
        res = dot3(hi_ref[a, :], lo_ref[a, :], vh, vl)
        for p in range(4):
            out[p * r:p * r + w, :] = res[p * w:(p + 1) * w, :]
        for j in range(k):
            a = slice(h * 128, (h + 1) * 128)
            res = dot3(prev[2 * j][a, :], prev[2 * j + 1][a, :], vh, vl)
            for p in range(4):
                o = p * r + w + 32 * j
                out[o:o + 32, :] = res[p * 32:(p + 1) * 32, :]
    if not last:
        th_ref, tl_ref = outs[4:6]
        vt = vbuf[...].T
        vbuf[0:256, :] = vt[:, 0:256]
        vbuf[256:512, :] = vt[:, 256:512]
        vbuf[512:768, :] = vt[:, 512:768]
        vbuf[768:1024, :] = vt[:, 768:1024]
        for p in range(8):
            for m in range(4):
                v = vbuf[pl.ds(pl.multiple_of(m * 256 + piece[p] * 32, 32), 32), :]
                h, l = split(v)
                th_ref[p * 32:(p + 1) * 32, m * 256:(m + 1) * 256] = h
                tl_ref[p * 32:(p + 1) * 32, m * 256:(m + 1) * 256] = l


def project(k, piece, block, b, c, hi, lo, prev):
    last = k == NREF - 1
    rows, nb = 2 * b.shape[0], b.shape[1]
    cols = hi.shape[0]
    r = cols // 8 + 32 * k
    out = [jax.ShapeDtypeStruct((4 * r, nb), F32)] * 2 + [jax.ShapeDtypeStruct((rows, nb), BF)] * 2
    if not last:
        out += [jax.ShapeDtypeStruct((nb, rows), BF)] * 2
    vmem = pl.BlockSpec(memory_space=pltpu.VMEM)
    smem = pl.BlockSpec(memory_space=pltpu.SMEM)
    return pl.pallas_call(
        functools.partial(project_kernel, k, last),
        out_shape=out,
        in_specs=[smem, smem] + [vmem] * (4 + 2 * k),
        out_specs=[vmem] * len(out),
        scratch_shapes=[pltpu.VMEM((rows, nb), F32)],
        compiler_params=pltpu.CompilerParams(vmem_limit_bytes=24 << 20),
        cost_estimate=pl.CostEstimate(flops=6 * 8 * r * rows * nb, bytes_accessed=4 * rows * cols + 8 * rows * nb, transcendentals=0),
    )(piece, block, b, c, hi, lo, *prev)


def update_kernel(k, *refs):
    piece, own_ref, got_ref, vh_ref, vl_ref, t_ref, field_ref = refs[:7]
    prev = refs[7:7 + 2 * k]
    out_ref, sh_ref, sl_ref, wh_ref, wl_ref, g_ref, bh_ref, bl_ref = refs[7 + 2 * k:]
    n = pl.program_id(0)
    w = wh_ref.shape[0] // 8
    r = w + 32 * k
    last2 = (((1,), (1,)), ((), ()))

    @pl.when(n == 0)
    def _():
        for p in range(8):
            src = own_ref if p < 4 else got_ref
            o = (p % 4) * r
            q = piece[p]
            at = pl.ds(pl.multiple_of(q * w, 32), w)
            wh_ref[at, :], wl_ref[at, :] = split(src[o:o + w, :])
            for j in range(k):
                a = o + w + 32 * j
                g_ref[pl.ds(pl.multiple_of(j * 256 + q * 32, 32), 32), :] = src[a:a + 32, :]
        t = t_ref[...]
        at = lax.broadcasted_iota(jnp.int32, t.shape, 0)
        upto = lax.broadcasted_iota(jnp.int32, t.shape, 1)
        t = jnp.where(at <= upto, t, 0.0)
        bh_ref[0:256, :], bl_ref[0:256, :] = split(t.T)
        if k:
            th, tl = split(t)
            gh, gl = split(g_ref[0:256 * k, :])
            a = slice(256, 256 * (k + 1))
            bh_ref[a, :], bl_ref[a, :] = split(-dot3(gh, gl, th, tl, last2))
        b = slice(0, 256 * (k + 1))
        ah = jnp.concatenate([wh_ref[...]] + [v[...] for v in prev[0::2]], axis=1)
        al = jnp.concatenate([wl_ref[...]] + [v[...] for v in prev[1::2]], axis=1)
        sh_ref[...], sl_ref[...] = split(dot3(ah, al, bh_ref[b, :], bl_ref[b, :]))

    tile = field_ref.shape[1]
    a = pl.ds(pl.multiple_of(n * tile, tile), tile)
    out_ref[...] = field_ref[...] - dot3(vh_ref[...], vl_ref[...], sh_ref[a, :], sl_ref[a, :], last2)


def update(k, piece, own, got, vh, vl, t, field, prev):
    rows, cols = field.shape
    nb = vh.shape[1]
    tile = 256
    full = lambda a: pl.BlockSpec(a.shape, lambda n: (0, 0))
    smem = pl.BlockSpec(memory_space=pltpu.SMEM)
    cut = pl.BlockSpec((rows, tile), lambda n: (0, n))
    sdef = jax.ShapeDtypeStruct((cols, nb), BF)
    scratch = [(cols, nb, BF)] * 2 + [(512, nb, F32)] + [(768, nb, BF)] * 2
    return pl.pallas_call(
        functools.partial(update_kernel, k),
        grid=(cols // tile,),
        out_shape=[jax.ShapeDtypeStruct(field.shape, F32), sdef, sdef],
        in_specs=[smem, full(own), full(got), full(vh), full(vl), full(t), cut] + [full(a) for a in prev],
        out_specs=[cut, full(sdef), full(sdef)],
        scratch_shapes=[pltpu.VMEM(s[:2], s[2]) for s in scratch],
        compiler_params=pltpu.CompilerParams(vmem_limit_bytes=32 << 20),
        cost_estimate=pl.CostEstimate(flops=6 * rows * cols * nb, bytes_accessed=8 * rows * cols, transcendentals=0),
    )(piece, own, got, vh, vl, t, field, *prev)


def steps(eigvec, panels, factors):
    piece_t, block_t = tables()
    row, col = lax.axis_index("row"), lax.axis_index("col")
    piece = jnp.asarray(piece_t)[row]
    block = jnp.asarray(block_t)[row % 2, col]

    def spread(v):
        return [v] + [send(v, ZL[d]) for d in (1, 2, 3)]

    first = spread(panels[0])
    rest = spread(panels[1:])
    hi, lo = prep(piece, eigvec)
    vs, ts, ws = [], [], []
    for k in range(NREF):
        a = jnp.concatenate(first if k == 0 else [v[k - 1] for v in rest], axis=0)
        b = send(a, X1)
        b = jnp.concatenate([a, b], axis=0)
        c = send(b, X2)
        keep, give, vh, vl, *t = project(k, piece, block, b, c, hi, lo, [u for pair in ts for u in pair])
        vs.append((vh, vl))
        if t:
            ts.append(t)
        w = send(give, CORE)
        w = keep + w
        h = w.shape[0] // 2
        u = send(w[h:], Y1)
        w = w[:h] + u
        u = send(w[h // 2:], Y2)
        w = w[:h // 2] + u
        u = send(w, ZH)
        w = w + u
        u = send(w, Y2)
        w = jnp.concatenate([w, u], axis=0)
        u = send(w, Y1)
        w = jnp.concatenate([w, u], axis=0)
        ws.append((w, send(w, CORE)))
    field = eigvec
    ss = []
    for k in range(NREF):
        field, *s = update(k, piece, *ws[k], *vs[k], factors[k], field, [u for pair in ss for u in pair])
        ss.append(s)
    return field


def solution(mesh):
    in_specs = (P("row", "col"), P(None, ("row", "col"), None), P())
    out_specs = P("row", "col")
    return jax.shard_map(steps, mesh=mesh, in_specs=in_specs, out_specs=out_specs, check_vma=False)
```

```python
import functools

import jax
import jax.numpy as jnp
import numpy as np
from jax import lax
from jax.experimental import pallas as pl
from jax.experimental.pallas import tpu as pltpu
from jax.sharding import PartitionSpec as P


NREF = 3
BF = jnp.bfloat16
F32 = jnp.float32


def lin(y, zh, c, x, zl):
    return ((y * 2 + zh) * 2 + c) * 16 + x * 4 + zl


def xor_pair(core):
    return (1, 3) if core == 0 else (3, 1)


def perm_of(f):
    pairs = []
    for y in range(4):
        for zh in range(2):
            for c in range(2):
                for x in range(4):
                    for zl in range(4):
                        pairs.append((lin(y, zh, c, x, zl), lin(*f(y, zh, c, x, zl))))
    return pairs


CORE = perm_of(lambda y, zh, c, x, zl: (y, zh, 1 - c, x, zl))
Y1 = perm_of(lambda y, zh, c, x, zl: (y ^ xor_pair(c)[0], zh, c, x, zl))
Y2 = perm_of(lambda y, zh, c, x, zl: (y ^ xor_pair(c)[1], zh, c, x, zl))
X1 = perm_of(lambda y, zh, c, x, zl: (y, zh, c, x ^ xor_pair(c)[0], zl))
X2 = perm_of(lambda y, zh, c, x, zl: (y, zh, c, x ^ xor_pair(c)[1], zl))
ZH = perm_of(lambda y, zh, c, x, zl: (y, 1 - zh, c, x, zl))
ZL = [perm_of(lambda y, zh, c, x, zl, d=d: (y, zh, c, x, zl ^ d)) for d in range(4)]


def send(a, perm):
    return lax.ppermute(a, ("row", "col"), perm)


def tables():
    piece = np.zeros((16, 8), np.int32)
    block = np.zeros((2, 16, 2, 16), np.int32)
    for r in range(16):
        y, c = r // 4, r % 2
        for p in range(8):
            b0, b1, b2 = p // 4, (p // 2) % 2, p % 2
            owner = c ^ b0
            g = xor_pair(owner)
            piece[r, p] = owner * 4 + (y ^ (b1 * g[0]) ^ (b2 * g[1]))
    for c in range(2):
        g = xor_pair(c)
        for j in range(16):
            x, zl = j // 4, j % 4
            for p in range(16):
                b2, b1, zp = p // 8, (p // 4) % 2, p % 4
                block[c, j, 0, p] = (x ^ (b1 * g[0]) ^ (b2 * g[1])) * 4 + (zl ^ zp)
                zp, b2, b1 = p // 4, (p // 2) % 2, p % 2
                block[c, j, 1, p] = (x ^ (b1 * g[0]) ^ (b2 * g[1])) * 4 + (zl ^ zp)
    return piece, block


def split(v):
    hi = v.astype(BF)
    return hi, (v - hi.astype(F32)).astype(BF)


def dot3(ah, al, bh, bl, dims=(((1,), (0,)), ((), ()))):
    d = functools.partial(lax.dot_general, dimension_numbers=dims, preferred_element_type=F32)
    return d(ah, bh) + (d(ah, bl) + d(al, bh))


def prep_kernel(piece, field_ref, hi_ref, lo_ref, buf):
    w = field_ref.shape[1] // 8
    tile = buf.shape[-1]

    @pl.loop(0, field_ref.shape[0] // tile)
    def _(n):
        b = pl.ds(pl.multiple_of(n * tile, tile), tile)
        buf[...] = field_ref[b, :].T
        for p in range(8):
            v = buf[pl.ds(pl.multiple_of(piece[p] * w, 32), w), :]
            a = slice(p * w, (p + 1) * w)
            hi_ref[a, b], lo_ref[a, b] = split(v)


def prep(piece, field):
    rows, cols = field.shape
    return pl.pallas_call(
        prep_kernel,
        out_shape=[jax.ShapeDtypeStruct((cols, rows), BF)] * 2,
        in_specs=[pl.BlockSpec(memory_space=pltpu.SMEM), pl.BlockSpec(memory_space=pltpu.VMEM)],
        out_specs=[pl.BlockSpec(memory_space=pltpu.VMEM)] * 2,
        scratch_shapes=[pltpu.VMEM((cols, 256), F32)],
        compiler_params=pltpu.CompilerParams(vmem_limit_bytes=24 << 20),
        cost_estimate=pl.CostEstimate(flops=0, bytes_accessed=rows * cols * 8, transcendentals=0),
        name="prep",
    )(piece, field)


def project_kernel(k, last, parts, *refs):
    piece, block = refs[:2]
    blocks = refs[2:2 + parts]
    hi_ref, lo_ref = refs[2 + parts:4 + parts]
    prev = refs[4 + parts:4 + parts + 2 * k]
    outs = refs[4 + parts + 2 * k:]
    keep_ref, give_ref, vh_ref, vl_ref = outs[:4]
    vbuf = outs[-1]
    at = 0
    for src in blocks:
        for o in range(0, src.shape[0], 64):
            vbuf[pl.ds(pl.multiple_of(block[at] * 64, 64), 64), :] = src[o:o + 64, :]
            at += 1
    vh_ref[...], vl_ref[...] = split(vbuf[...])
    vh, vl = vh_ref[...], vl_ref[...]
    w = hi_ref.shape[0] // 8
    r = w + 32 * k

    def side(h, refs):
        a = pl.ds(pl.multiple_of(h * 4 * w, 32), 4 * w)
        res = dot3(hi_ref[a, :], lo_ref[a, :], vh, vl)
        a = pl.ds(pl.multiple_of(h * 128, 128), 128)
        more = [dot3(prev[2 * j][a, :], prev[2 * j + 1][a, :], vh, vl) for j in range(k)]

        def store(out):
            for p in range(4):
                out[p * r:p * r + w, :] = res[p * w:(p + 1) * w, :]
                for j in range(k):
                    o = p * r + w + 32 * j
                    out[o:o + 32, :] = more[j][p * 32:(p + 1) * 32, :]

        for g, out in refs:
            if len(refs) == 1:
                store(out)
            else:
                pl.when(h == g)(functools.partial(store, out))

    if k == 0:
        pl.loop(0, 2)(lambda h: side(h, ((0, keep_ref), (1, give_ref))))
    else:
        side(1, ((1, give_ref),))
        side(0, ((0, keep_ref),))
    if not last:
        th_ref, tl_ref = outs[4:6]
        vt = vbuf[...].T
        vbuf[0:256, :] = vt[:, 0:256]
        vbuf[256:512, :] = vt[:, 256:512]
        vbuf[512:768, :] = vt[:, 512:768]
        vbuf[768:1024, :] = vt[:, 768:1024]

        @pl.loop(0, 8)
        def _(p):
            to = pl.ds(pl.multiple_of(p * 32, 32), 32)
            for m in range(4):
                v = vbuf[pl.ds(pl.multiple_of(m * 256 + piece[p] * 32, 32), 32), :]
                b = slice(m * 256, (m + 1) * 256)
                th_ref[to, b], tl_ref[to, b] = split(v)


def project(k, piece, block, parts, hi, lo, prev):
    last = k == NREF - 1
    rows, nb = sum(v.shape[0] for v in parts), parts[0].shape[1]
    cols = hi.shape[0]
    r = cols // 8 + 32 * k
    out = [jax.ShapeDtypeStruct((4 * r, nb), F32)] * 2 + [jax.ShapeDtypeStruct((rows, nb), BF)] * 2
    if not last:
        out += [jax.ShapeDtypeStruct((nb, rows), BF)] * 2
    vmem = pl.BlockSpec(memory_space=pltpu.VMEM)
    smem = pl.BlockSpec(memory_space=pltpu.SMEM)
    return pl.pallas_call(
        functools.partial(project_kernel, k, last, len(parts)),
        out_shape=out,
        in_specs=[smem, smem] + [vmem] * (2 + len(parts) + 2 * k),
        out_specs=[vmem] * len(out),
        scratch_shapes=[pltpu.VMEM((rows, nb), F32)],
        compiler_params=pltpu.CompilerParams(vmem_limit_bytes=24 << 20),
        cost_estimate=pl.CostEstimate(flops=6 * 8 * r * rows * nb, bytes_accessed=4 * rows * cols + 8 * rows * nb, transcendentals=0),
    )(piece, block, *parts, hi, lo, *prev)


def update_kernel(k, last, *refs):
    piece, own_ref, got_ref, vh_ref, vl_ref, t_ref, field_ref = refs[:7]
    prev = refs[7:7 + 2 * k]
    if last:
        out_ref, wh_ref, wl_ref, g_ref, bh_ref, bl_ref, done, sems = refs[7 + 2 * k:]
    else:
        out_ref, sh_ref, sl_ref, wh_ref, wl_ref, g_ref, bh_ref, bl_ref = refs[7 + 2 * k:]
    cols = wh_ref.shape[0]
    w = cols // 8
    r = w + 32 * k
    last2 = (((1,), (1,)), ((), ()))
    t = t_ref[...]
    at = lax.broadcasted_iota(jnp.int32, t.shape, 0)
    upto = lax.broadcasted_iota(jnp.int32, t.shape, 1)
    t = jnp.where(at <= upto, t, 0.0)
    bh_ref[0:256, :], bl_ref[0:256, :] = split(t.T)
    for p in range(8):
        src = own_ref if p < 4 else got_ref
        for j in range(k):
            a = (p % 4) * r + w + 32 * j
            g_ref[pl.ds(pl.multiple_of(j * 256 + piece[p] * 32, 32), 32), :] = src[a:a + 32, :]
    if k:
        th, tl = split(t)
        gh, gl = split(g_ref[0:256 * k, :])
        a = slice(256, 256 * (k + 1))
        bh_ref[a, :], bl_ref[a, :] = split(-dot3(gh, gl, th, tl, last2))
    for base, src in ((0, own_ref), (4, got_ref)):

        def place(p, base=base, src=src):
            a = pl.ds(pl.multiple_of(piece[base + p] * w, 32), w)
            wh_ref[a, :], wl_ref[a, :] = split(src[pl.ds(pl.multiple_of(p * r, 32), w), :])

        if last:
            for p in range(4):
                place(p)
        else:
            pl.loop(0, 4)(place)
    b = slice(0, 256 * (k + 1))
    tile = 256

    def store(n):
        to = slice(n * tile, (n + 1) * tile)
        return pltpu.make_async_copy(done.at[n], out_ref.at[:, to], sems.at[n])

    def step(n):
        a = pl.ds(pl.multiple_of(n * tile, tile), tile) if k == 0 else slice(n * tile, (n + 1) * tile)
        ah = jnp.concatenate([wh_ref[a, :]] + [v[a, :] for v in prev[0::2]], axis=1)
        al = jnp.concatenate([wl_ref[a, :]] + [v[a, :] for v in prev[1::2]], axis=1)
        sh, sl = split(dot3(ah, al, bh_ref[b, :], bl_ref[b, :]))
        if not last:
            sh_ref[a, :], sl_ref[a, :] = sh, sl
        res = field_ref[:, a] - dot3(vh_ref[...], vl_ref[...], sh, sl, last2)
        if last:
            done[n] = res
            store(n).start()
        else:
            out_ref[:, a] = res

    if k == 0:
        pl.loop(0, cols // tile)(step)
    else:
        for n in range(cols // tile):
            step(n)
    if last:
        for n in range(cols // tile):
            store(n).wait()


def update(k, piece, own, got, vh, vl, t, field, prev):
    last = k == NREF - 1
    rows, cols = field.shape
    nb = vh.shape[1]
    smem = pl.BlockSpec(memory_space=pltpu.SMEM)
    vmem = pl.BlockSpec(memory_space=pltpu.VMEM)
    sdef = jax.ShapeDtypeStruct((cols, nb), BF)
    scratch = [(cols, nb, BF)] * 2 + [(512, nb, F32)] + [(768, nb, BF)] * 2
    scratch = [pltpu.VMEM(s[:2], s[2]) for s in scratch]
    if last:
        scratch += [pltpu.VMEM((cols // 256, rows, 256), F32), pltpu.SemaphoreType.DMA((cols // 256,))]
    return pl.pallas_call(
        functools.partial(update_kernel, k, last),
        out_shape=[jax.ShapeDtypeStruct(field.shape, F32)] + [sdef] * (0 if last else 2),
        in_specs=[smem] + [vmem] * (6 + len(prev)),
        out_specs=[pl.BlockSpec(memory_space=pltpu.HBM)] if last else [vmem] * 3,
        scratch_shapes=scratch,
        compiler_params=pltpu.CompilerParams(vmem_limit_bytes=32 << 20),
        cost_estimate=pl.CostEstimate(flops=6 * rows * cols * nb, bytes_accessed=8 * rows * cols, transcendentals=0),
    )(piece, own, got, vh, vl, t, field, *prev)


def steps(eigvec, panels, factors):
    piece_t, block_t = tables()
    row, col = lax.axis_index("row"), lax.axis_index("col")
    piece = jnp.asarray(piece_t)[row]
    blocks = jnp.asarray(block_t)[row % 2, col]

    def over_x(v):
        u = send(v, X1)
        v = jnp.concatenate([v, u], axis=0)
        return v, send(v, X2)

    def over_z(v):
        return [v] + [send(v, ZL[d]) for d in (1, 2, 3)]

    first = over_z(panels[0])
    second = over_z(panels[1])
    hi, lo = prep(piece, eigvec)
    vs, ts, ws = [], [], []
    for k in range(NREF):
        if k < 2:
            a = jnp.concatenate([first, second][k], axis=0)
            parts, block = over_x(a), blocks[0]
        else:
            a = over_x(panels[2])
            a = jnp.concatenate(a, axis=0)
            parts, block = over_z(a), blocks[1]
        keep, give, vh, vl, *t = project(k, piece, block, parts, hi, lo, [u for pair in ts for u in pair])
        vs.append((vh, vl))
        if t:
            ts.append(t)
        w = send(give, CORE)
        w = keep + w
        h = w.shape[0] // 2
        u = send(w[h:], Y1)
        w = w[:h] + u
        u = send(w[h // 2:], Y2)
        w = w[:h // 2] + u
        u = send(w, ZH)
        w = w + u
        u = send(w, Y2)
        w = jnp.concatenate([w, u], axis=0)
        u = send(w, Y1)
        w = jnp.concatenate([w, u], axis=0)
        ws.append((w, send(w, CORE)))
    field = eigvec
    ss = []
    for k in range(NREF):
        field, *s = update(k, piece, *ws[k], *vs[k], factors[k], field, [u for pair in ss for u in pair])
        ss.append(s)
    return field


def solution(mesh):
    in_specs = (P("row", "col"), P(None, ("row", "col"), None), P())
    out_specs = P("row", "col")
    return jax.shard_map(steps, mesh=mesh, in_specs=in_specs, out_specs=out_specs, check_vma=False)
```

```python
import functools

import jax
import jax.numpy as jnp
import numpy as np
from jax import lax
from jax.experimental import pallas as pl
from jax.experimental.pallas import tpu as pltpu
from jax.sharding import PartitionSpec as P


NREF = 3
BF = jnp.bfloat16
F32 = jnp.float32


def lin(y, zh, c, x, zl):
    return ((y * 2 + zh) * 2 + c) * 16 + x * 4 + zl


def xor_pair(core):
    return (1, 3) if core == 0 else (3, 1)


def perm_of(f):
    pairs = []
    for y in range(4):
        for zh in range(2):
            for c in range(2):
                for x in range(4):
                    for zl in range(4):
                        pairs.append((lin(y, zh, c, x, zl), lin(*f(y, zh, c, x, zl))))
    return pairs


CORE = perm_of(lambda y, zh, c, x, zl: (y, zh, 1 - c, x, zl))
Y1 = perm_of(lambda y, zh, c, x, zl: (y ^ xor_pair(c)[0], zh, c, x, zl))
Y2 = perm_of(lambda y, zh, c, x, zl: (y ^ xor_pair(c)[1], zh, c, x, zl))
X1 = perm_of(lambda y, zh, c, x, zl: (y, zh, c, x ^ xor_pair(c)[0], zl))
X2 = perm_of(lambda y, zh, c, x, zl: (y, zh, c, x ^ xor_pair(c)[1], zl))
ZH = perm_of(lambda y, zh, c, x, zl: (y, 1 - zh, c, x, zl))
ZL = [perm_of(lambda y, zh, c, x, zl, d=d: (y, zh, c, x, zl ^ d)) for d in range(4)]


def send(a, perm):
    return lax.ppermute(a, ("row", "col"), perm)


def tables():
    piece = np.zeros((16, 8), np.int32)
    block = np.zeros((2, 16, 2, 16), np.int32)
    for r in range(16):
        y, c = r // 4, r % 2
        for p in range(8):
            b0, b1, b2 = p // 4, (p // 2) % 2, p % 2
            owner = c ^ b0
            g = xor_pair(owner)
            piece[r, p] = owner * 4 + (y ^ (b1 * g[0]) ^ (b2 * g[1]))
    for c in range(2):
        g = xor_pair(c)
        for j in range(16):
            x, zl = j // 4, j % 4
            for p in range(16):
                b2, b1, zp = p // 8, (p // 4) % 2, p % 4
                block[c, j, 0, p] = (x ^ (b1 * g[0]) ^ (b2 * g[1])) * 4 + (zl ^ zp)
                zp, b2, b1 = p // 4, (p // 2) % 2, p % 2
                block[c, j, 1, p] = (x ^ (b1 * g[0]) ^ (b2 * g[1])) * 4 + (zl ^ zp)
    return piece, block


def split(v):
    hi = v.astype(BF)
    return hi, (v - hi.astype(F32)).astype(BF)


def dot3(ah, al, bh, bl, dims=(((1,), (0,)), ((), ()))):
    d = functools.partial(lax.dot_general, dimension_numbers=dims, preferred_element_type=F32)
    return d(ah, bh) + (d(ah, bl) + d(al, bh))


def prep_kernel(piece, field_ref, hi_ref, lo_ref, buf):
    w = field_ref.shape[1] // 8
    tile = buf.shape[-1]

    @pl.loop(0, field_ref.shape[0] // tile)
    def _(n):
        b = pl.ds(pl.multiple_of(n * tile, tile), tile)
        buf[...] = field_ref[b, :].T
        for p in range(8):
            v = buf[pl.ds(pl.multiple_of(piece[p] * w, 32), w), :]
            a = slice(p * w, (p + 1) * w)
            hi_ref[a, b], lo_ref[a, b] = split(v)


def prep(piece, field):
    rows, cols = field.shape
    return pl.pallas_call(
        prep_kernel,
        out_shape=[jax.ShapeDtypeStruct((cols, rows), BF)] * 2,
        in_specs=[pl.BlockSpec(memory_space=pltpu.SMEM), pl.BlockSpec(memory_space=pltpu.VMEM)],
        out_specs=[pl.BlockSpec(memory_space=pltpu.VMEM)] * 2,
        scratch_shapes=[pltpu.VMEM((cols, 128), F32)],
        compiler_params=pltpu.CompilerParams(vmem_limit_bytes=24 << 20),
        cost_estimate=pl.CostEstimate(flops=0, bytes_accessed=rows * cols * 8, transcendentals=0),
        name="prep",
    )(piece, field)


def project_kernel(k, last, parts, *refs):
    piece, block = refs[:2]
    blocks = refs[2:2 + parts]
    hi_ref, lo_ref = refs[2 + parts:4 + parts]
    prev = refs[4 + parts:4 + parts + 2 * k]
    outs = refs[4 + parts + 2 * k:]
    keep_ref, give_ref, vh_ref, vl_ref = outs[:4]
    vbuf = outs[-1]
    at = 0
    for src in blocks:
        for o in range(0, src.shape[0], 64):
            vbuf[pl.ds(pl.multiple_of(block[at] * 64, 64), 64), :] = src[o:o + 64, :]
            at += 1

    @pl.loop(0, vbuf.shape[0] // 64)
    def _(o):
        a = pl.ds(pl.multiple_of(o * 64, 64), 64)
        vh_ref[a, :], vl_ref[a, :] = split(vbuf[a, :])

    vh, vl = vh_ref[...], vl_ref[...]
    w = hi_ref.shape[0] // 8
    r = w + 32 * k

    def side(h, refs):
        a = pl.ds(pl.multiple_of(h * 4 * w, 32), 4 * w)
        res = dot3(hi_ref[a, :], lo_ref[a, :], vh, vl)
        a = pl.ds(pl.multiple_of(h * 128, 128), 128)
        more = [dot3(prev[2 * j][a, :], prev[2 * j + 1][a, :], vh, vl) for j in range(k)]

        def store(out):
            for p in range(4):
                out[p * r:p * r + w, :] = res[p * w:(p + 1) * w, :]
                for j in range(k):
                    o = p * r + w + 32 * j
                    out[o:o + 32, :] = more[j][p * 32:(p + 1) * 32, :]

        for g, out in refs:
            if len(refs) == 1:
                store(out)
            else:
                pl.when(h == g)(functools.partial(store, out))

    side(1, ((1, give_ref),))
    side(0, ((0, keep_ref),))
    if not last:
        th_ref, tl_ref = outs[4:6]
        vt = vbuf[...].T
        vbuf[0:256, :] = vt[:, 0:256]
        vbuf[256:512, :] = vt[:, 256:512]
        vbuf[512:768, :] = vt[:, 512:768]
        vbuf[768:1024, :] = vt[:, 768:1024]

        @pl.loop(0, 8)
        def _(p):
            to = pl.ds(pl.multiple_of(p * 32, 32), 32)
            for m in range(4):
                v = vbuf[pl.ds(pl.multiple_of(m * 256 + piece[p] * 32, 32), 32), :]
                b = slice(m * 256, (m + 1) * 256)
                th_ref[to, b], tl_ref[to, b] = split(v)


def project(k, piece, block, parts, hi, lo, prev):
    last = k == NREF - 1
    rows, nb = sum(v.shape[0] for v in parts), parts[0].shape[1]
    cols = hi.shape[0]
    r = cols // 8 + 32 * k
    out = [jax.ShapeDtypeStruct((4 * r, nb), F32)] * 2 + [jax.ShapeDtypeStruct((rows, nb), BF)] * 2
    if not last:
        out += [jax.ShapeDtypeStruct((nb, rows), BF)] * 2
    vmem = pl.BlockSpec(memory_space=pltpu.VMEM)
    smem = pl.BlockSpec(memory_space=pltpu.SMEM)
    return pl.pallas_call(
        functools.partial(project_kernel, k, last, len(parts)),
        out_shape=out,
        in_specs=[smem, smem] + [vmem] * (2 + len(parts) + 2 * k),
        out_specs=[vmem] * len(out),
        scratch_shapes=[pltpu.VMEM((rows, nb), F32)],
        compiler_params=pltpu.CompilerParams(vmem_limit_bytes=24 << 20),
        cost_estimate=pl.CostEstimate(flops=6 * 8 * r * rows * nb, bytes_accessed=4 * rows * cols + 8 * rows * nb, transcendentals=0),
    )(piece, block, *parts, hi, lo, *prev)


def update_kernel(k, last, *refs):
    piece, own_ref, got_ref, vh_ref, vl_ref, t_ref, field_ref = refs[:7]
    prev = refs[7:7 + 2 * k]
    if last:
        out_ref, wh_ref, wl_ref, g_ref, bh_ref, bl_ref, done, sems = refs[7 + 2 * k:]
    else:
        out_ref, sh_ref, sl_ref, wh_ref, wl_ref, g_ref, bh_ref, bl_ref = refs[7 + 2 * k:]
    cols = wh_ref.shape[0]
    w = cols // 8
    r = w + 32 * k
    last2 = (((1,), (1,)), ((), ()))
    t = t_ref[...]
    at = lax.broadcasted_iota(jnp.int32, t.shape, 0)
    upto = lax.broadcasted_iota(jnp.int32, t.shape, 1)
    t = jnp.where(at <= upto, t, 0.0)
    bh_ref[0:256, :], bl_ref[0:256, :] = split(t.T)
    for p in range(8):
        src = own_ref if p < 4 else got_ref
        for j in range(k):
            a = (p % 4) * r + w + 32 * j
            g_ref[pl.ds(pl.multiple_of(j * 256 + piece[p] * 32, 32), 32), :] = src[a:a + 32, :]
    if k:
        th, tl = split(t)
        gh, gl = split(g_ref[0:256 * k, :])
        a = slice(256, 256 * (k + 1))
        bh_ref[a, :], bl_ref[a, :] = split(-dot3(gh, gl, th, tl, last2))
    for base, src in ((0, own_ref), (4, got_ref)):

        def place(p, base=base, src=src):
            a = pl.ds(pl.multiple_of(piece[base + p] * w, 32), w)
            wh_ref[a, :], wl_ref[a, :] = split(src[pl.ds(pl.multiple_of(p * r, 32), w), :])

        pl.loop(0, 4)(place)
    b = slice(0, 256 * (k + 1))
    tile = 256

    def store(n):
        to = slice(n * tile, (n + 1) * tile)
        return pltpu.make_async_copy(done.at[n], out_ref.at[:, to], sems.at[n])

    def step(n):
        a = slice(n * tile, (n + 1) * tile)
        ah = jnp.concatenate([wh_ref[a, :]] + [v[a, :] for v in prev[0::2]], axis=1)
        al = jnp.concatenate([wl_ref[a, :]] + [v[a, :] for v in prev[1::2]], axis=1)
        sh, sl = split(dot3(ah, al, bh_ref[b, :], bl_ref[b, :]))
        if not last:
            sh_ref[a, :], sl_ref[a, :] = sh, sl
        res = field_ref[:, a] - dot3(vh_ref[...], vl_ref[...], sh, sl, last2)
        if last:
            done[n] = res
            store(n).start()
        else:
            out_ref[:, a] = res

    for n in range(cols // tile):
        step(n)
    if last:
        for n in range(cols // tile):
            store(n).wait()


def update(k, piece, own, got, vh, vl, t, field, prev):
    last = k == NREF - 1
    rows, cols = field.shape
    nb = vh.shape[1]
    smem = pl.BlockSpec(memory_space=pltpu.SMEM)
    vmem = pl.BlockSpec(memory_space=pltpu.VMEM)
    sdef = jax.ShapeDtypeStruct((cols, nb), BF)
    scratch = [(cols, nb, BF)] * 2 + [(512, nb, F32)] + [(768, nb, BF)] * 2
    scratch = [pltpu.VMEM(s[:2], s[2]) for s in scratch]
    if last:
        scratch += [pltpu.VMEM((cols // 256, rows, 256), F32), pltpu.SemaphoreType.DMA((cols // 256,))]
    return pl.pallas_call(
        functools.partial(update_kernel, k, last),
        out_shape=[jax.ShapeDtypeStruct(field.shape, F32)] + [sdef] * (0 if last else 2),
        in_specs=[smem] + [vmem] * (6 + len(prev)),
        out_specs=[pl.BlockSpec(memory_space=pltpu.HBM)] if last else [vmem] * 3,
        scratch_shapes=scratch,
        compiler_params=pltpu.CompilerParams(vmem_limit_bytes=32 << 20),
        cost_estimate=pl.CostEstimate(flops=6 * rows * cols * nb, bytes_accessed=8 * rows * cols, transcendentals=0),
    )(piece, own, got, vh, vl, t, field, *prev)


def steps(eigvec, panels, factors):
    piece_t, block_t = tables()
    row, col = lax.axis_index("row"), lax.axis_index("col")
    piece = jnp.asarray(piece_t)[row]
    blocks = jnp.asarray(block_t)[row % 2, col]

    def over_x(v):
        u = send(v, X1)
        v = jnp.concatenate([v, u], axis=0)
        return v, send(v, X2)

    def over_z(v):
        return [v] + [send(v, ZL[d]) for d in (1, 2, 3)]

    first = over_z(panels[0])
    second = over_z(panels[1])
    hi, lo = prep(piece, eigvec)
    vs, ts, ws = [], [], []
    for k in range(NREF):
        if k < 2:
            a = jnp.concatenate([first, second][k], axis=0)
            parts, block = over_x(a), blocks[0]
        else:
            a = over_x(panels[2])
            a = jnp.concatenate(a, axis=0)
            parts, block = over_z(a), blocks[1]
        keep, give, vh, vl, *t = project(k, piece, block, parts, hi, lo, [u for pair in ts for u in pair])
        vs.append((vh, vl))
        if t:
            ts.append(t)
        w = send(give, CORE)
        w = keep + w
        h = w.shape[0] // 2
        u = send(w[h:], Y1)
        w = w[:h] + u
        u = send(w[h // 2:], Y2)
        w = w[:h // 2] + u
        u = send(w, ZH)
        w = w + u
        u = send(w, Y2)
        w = jnp.concatenate([w, u], axis=0)
        u = send(w, Y1)
        w = jnp.concatenate([w, u], axis=0)
        ws.append((w, send(w, CORE)))
    field = eigvec
    ss = []
    for k in range(NREF):
        field, *s = update(k, piece, *ws[k], *vs[k], factors[k], field, [u for pair in ss for u in pair])
        ss.append(s)
    return field


def solution(mesh):
    in_specs = (P("row", "col"), P(None, ("row", "col"), None), P())
    out_specs = P("row", "col")
    return jax.shard_map(steps, mesh=mesh, in_specs=in_specs, out_specs=out_specs, check_vma=False)
```
